32 devices in a mesh: space: 8 (over z, x), sub: 4 (over y, core).
Axes of the slice: x: 2, y: 2, z: 4, core: 2. Of those that a mesh axis runs over, the one named last changes fastest.
Arguments:
- multipole: float32 [8192, 152], P('space'), may hold values from -6 to 6
- inherited: float32 [8192, 152], P(('space', 'sub')), may hold values from -6 to 6
- send_rows: int32 [8, 4, 384], P('space'), may hold values from 0 to 1023
- sources: int32 [8192, 316], P('space', 'sub'), may hold values from -1 to 2559, as said below
- operators: float32 [316, 152, 152], P('sub'), may hold values from -0.0546875 to 0.0546875
Outputs:
- local: float32 [8192, 152], P(('space', 'sub'))
The draws below stay inside these ranges and needn't reach their ends.
Inputs may be any that keep to these rules, and one draw needn't show every extreme that they name: `sources`: an entry that names a ghost row names one whose sending block exists.
All inputs are finite; a program needn't handle non-finite values.
Results may differ from the reference program's by a relative error of at most 0.0003.
Values sent between devices are 32-bit elements; how exact they have to be, the bound alone decides.
A program may use at most 192 MiB of HBM per device.

```python
import jax
import jax.numpy as jnp
from jax import lax

COEF = 152
OPS_DEV = 79
OPS = 316
C_DEV = 1024
GH = 384
NEAR = 2
CELLS = 8192
BLOCKS = 8
N_SPACE = 8
N_SUB = 4


def draw_sources(key, part):
    keys = jax.random.split(key, 5)
    shape = (C_DEV * N_SPACE, OPS_DEV * N_SUB)
    present = jax.random.randint(keys[0], shape, 0, 10) < 6
    ghostly = jax.random.randint(keys[1], shape, 0, 2) == 1
    local_row = jax.random.randint(keys[2], shape, 0, C_DEV)
    peer_slot = jax.random.randint(keys[3], shape, 0, 2 * NEAR)
    slot_index = jax.random.randint(keys[4], shape, 0, GH)
    device = (jnp.arange(shape[0], dtype=jnp.int32) // C_DEV)[:, None]
    offset = jnp.where(peer_slot < NEAR, peer_slot + 1, NEAR - 1 - peer_slot)
    anchor = device - offset
    reachable = (anchor >= 0) & (anchor < N_SPACE)
    ghost_index = C_DEV + peer_slot * GH + slot_index
    value = jnp.where(ghostly, ghost_index, local_row)
    keep = present & (reachable | jnp.logical_not(ghostly))
    return jnp.where(keep, value, -1).astype(jnp.int32)


def plant(array, rng, smallest, top_value):
    longest = array.shape.index(max(array.shape))
    spots = []
    for shift in (0, 1):
        where = [jax.random.randint(jax.random.fold_in(rng, axis), (), 0, length) for axis, length in enumerate(array.shape)]
        where[longest] = (where[longest] + shift) % array.shape[longest]
        spots.append(tuple(where))
    return array.at[spots[0]].set(smallest).at[spots[1]].set(top_value)


def block_levels(rng, dims, cuts, least, high):
    def one(dim, parts):
        steps = jax.random.uniform(jax.random.fold_in(jax.random.fold_in(rng, 6), dim), (parts,), jnp.float32, least / len(cuts), high / len(cuts))
        return jnp.repeat(jnp.exp(steps), dims[dim] // parts).reshape((-1,) + (1,) * (len(dims) - dim - 1))

    gain = one(*cuts[0])
    for cut in cuts[1:]:
        gain = gain * one(*cut)
    return gain


def scatter_about(stream_key, shape, spread, most, shards=(), held_as=jnp.bfloat16):
    entries = jax.random.normal(stream_key, shape, jnp.float32) * spread
    if len(shards) > 0:
        entries = block_levels(stream_key, shape, shards, -0.22, 0.18) * entries
    return jnp.clip(entries, min=-most, max=most).astype(held_as)


def setup_inputs(seed: int = 0) -> dict:
    streams_of = jax.random.split(jax.random.key(seed), 6)
    multipole = scatter_about(streams_of[0], (CELLS, COEF), 1.0, 6.0, ((0, 8),), jnp.float32)
    inherited = scatter_about(streams_of[1], (CELLS, COEF), 1.0, 6.0, ((0, 32),), jnp.float32)
    send_rows = plant(jax.random.randint(streams_of[2], (BLOCKS, 2 * NEAR, GH), 0, C_DEV), jax.random.fold_in(streams_of[2], 1), 0, C_DEV - 1).astype(jnp.int32)
    sources = draw_sources(jax.random.fold_in(streams_of[5], 71), 0)
    operators = scatter_about(streams_of[4], (OPS, COEF, COEF), (COEF * OPS_DEV) ** -0.5, 0.0546875, ((0, 4),), jnp.float32)
    return dict(multipole=multipole, inherited=inherited, send_rows=send_rows, sources=sources, operators=operators)


def reference(multipole, inherited, send_rows, sources, operators):
    blocks = multipole.reshape(N_SPACE, C_DEV, COEF)
    flat_ops = operators.reshape(OPS_DEV * N_SUB * COEF, COEF)
    source_blocks = sources.reshape(N_SPACE, C_DEV, OPS_DEV * N_SUB)

    def one_device(pieces):
        device, index_block = pieces
        ghost_list = []
        for peer_slot in range(2 * NEAR):
            offset = peer_slot + 1 if peer_slot < NEAR else NEAR - 1 - peer_slot
            anchor = device - offset
            inside = (anchor >= 0) & (anchor < N_SPACE)
            safe_anchor = jnp.clip(anchor, 0, N_SPACE - 1).astype(jnp.int32)
            picked = blocks[safe_anchor][send_rows[safe_anchor, peer_slot]]
            ghost_list.append(jnp.where(inside, picked, jnp.zeros_like(picked)))
        lookup = jnp.concatenate([blocks[device]] + ghost_list, axis=0)
        present = index_block >= 0
        safe_index = jnp.where(present, index_block, 0).astype(jnp.int32)
        gathered = jnp.where(present[:, :, None], lookup[safe_index], jnp.zeros((), lookup.dtype))
        return jnp.dot(gathered.reshape(C_DEV, -1), flat_ops, precision=lax.Precision.HIGHEST, preferred_element_type=jnp.float32)

    partial_value = lax.map(one_device, (jnp.arange(N_SPACE, dtype=jnp.int32), source_blocks))
    return partial_value.reshape(C_DEV * N_SPACE, COEF) + inherited
```

```python
import functools

import jax
import jax.numpy as jnp
from jax import lax
from jax.experimental import pallas as pl
from jax.experimental.pallas import tpu as pltpu
from jax.sharding import PartitionSpec as P

LANES = 128
GROUP = LANES // 4
MESH = pl.DeviceIdType.MESH
PARTS = 4


def spread_rows(tail):
    pad = jnp.zeros((GROUP - tail.shape[0], tail.shape[1]), jnp.float32)
    end = jnp.zeros((GROUP, tail.shape[1]), jnp.float32)
    return jnp.concatenate([tail, pad, tail, pad, tail, pad, end], axis=0)


def weights(full, tail):
    high = full.astype(jnp.bfloat16).astype(jnp.float32)
    low = full - high
    pad = jnp.zeros((GROUP - tail, full.shape[1]), jnp.float32)
    end = jnp.zeros((GROUP, full.shape[1]), jnp.float32)
    mix = jnp.concatenate([high[LANES:], pad, high[LANES:], pad, low[LANES:], pad, end], axis=0)
    first = high[:LANES].astype(jnp.bfloat16)
    second = low[:LANES].astype(jnp.bfloat16)
    return jnp.concatenate([first, first, second, mix.astype(jnp.bfloat16)], axis=0)


def sources_part(head, rest):
    head_high = head.astype(jnp.bfloat16)
    head_low = (head - head_high.astype(jnp.float32)).astype(jnp.bfloat16)
    rest_high = rest.astype(jnp.bfloat16).astype(jnp.float32)
    lane = lax.broadcasted_iota(jnp.int32, rest.shape, 1)
    second = (lane >= GROUP) & (lane < 2 * GROUP)
    rest_mix = jnp.where(second, rest - rest_high, rest_high).astype(jnp.bfloat16)
    return jnp.concatenate([head_high, head_low, head_high, rest_mix], axis=1)


def exchange(
    dims, send_map, block, ops, table, w_head, w_tail, picked, stage, land, raw,
    raw_sems, ghost_send, ghost_recv,
):
    n_space, near, gh = dims
    width, rows = block.shape
    count = ops.shape[2]
    tail = width - LANES
    slots = 2 * near
    space, me = lax.axis_index("space"), lax.axis_index("sub")
    offsets = [j + 1 if j < near else near - 1 - j for j in range(slots)]
    flat = table.reshape(2 * table.shape[0], LANES)
    flat_picked = picked.reshape(2 * gh, LANES)

    per = width // PARTS
    raw_copies = []
    for k in range(PARTS):
        copy = pltpu.make_async_copy(
            ops.at[pl.ds(k * per, per)], raw.at[pl.ds(k * per, per)], raw_sems.at[k]
        )
        copy.start()
        raw_copies.append(copy)

    barrier = pltpu.get_barrier_semaphore()
    met = 0
    for offset in offsets:
        there = (space + offset >= 0) & (space + offset < n_space)
        met = met + there.astype(jnp.int32)

        @pl.when(there)
        def _():
            pl.semaphore_signal(barrier, inc=1, device_id=(space + offset, me), device_id_type=MESH)

    flat[pl.ds(0, rows, stride=2), :] = block[:LANES, :].T
    flat[pl.ds(1, rows, stride=2), :] = spread_rows(block[LANES:, :]).T
    first_free = 2 * (rows + slots * gh)
    flat[first_free:, :] = jnp.zeros((flat.shape[0] - first_free, LANES), jnp.float32)

    pl.semaphore_wait(barrier, met)

    quarter = gh // 4
    lane = lax.broadcasted_iota(jnp.int32, (quarter, LANES), 1)
    copies = []
    for j, offset in enumerate(offsets):
        there = (space + offset >= 0) & (space + offset < n_space)
        for g in range(gh):
            picked[g] = table[send_map[j * gh + g]]
        stage[j, :gh] = flat_picked[pl.ds(0, gh, stride=2), :]
        q = [flat_picked[pl.ds(2 * k * quarter + 1, quarter, stride=2), :] for k in range(4)]
        stage[j, gh:] = jnp.where(
            lane < GROUP,
            q[0],
            jnp.where(
                lane < 2 * GROUP,
                q[1],
                jnp.where(lane < 3 * GROUP, q[2], pltpu.roll(q[3], 3 * GROUP, 1)),
            ),
        )
        copy = pltpu.make_async_remote_copy(
            src_ref=stage.at[j],
            dst_ref=land.at[j],
            send_sem=ghost_send.at[j],
            recv_sem=ghost_recv.at[j],
            device_id=(jnp.clip(space + offset, 0, n_space - 1), me),
            device_id_type=MESH,
        )
        copies.append(copy)

        @pl.when(there)
        def _():
            copy.start()

    held = w_head.shape[0] // width

    for k in range(PARTS):
        raw_copies[k].wait()

        @pl.loop(k * per, (k + 1) * per, step=2)
        def _(i0):
            for u in range(2):
                i = i0 + u
                slab = raw[i]
                slab = jnp.concatenate(
                    [slab, jnp.zeros((width, LANES - count), jnp.float32)], axis=1
                )
                turned = slab.T
                w_head[pl.ds(i, held, stride=width), :] = turned[:held, :LANES]
                w_tail[pl.ds(i, held, stride=width), :] = jnp.concatenate(
                    [turned[:held, LANES:], jnp.zeros((held, LANES - tail), jnp.float32)], axis=1
                )

    for j, offset in enumerate(offsets):
        there = (space + offset >= 0) & (space + offset < n_space)
        here = (space - offset >= 0) & (space - offset < n_space)

        @pl.when(there)
        def _():
            copies[j].wait_send()

        @pl.when(here)
        def _():
            copies[j].wait_recv()
            base = 2 * (rows + j * gh)
            flat[pl.ds(base, gh, stride=2), :] = land[j, :gh]
            packed = land[j, gh:]
            turns = [packed] + [pltpu.roll(packed, d * GROUP, 1) for d in range(1, 4)]
            for k in range(4):
                spread = jnp.where(
                    lane < GROUP,
                    turns[(0 - k) % 4],
                    jnp.where(
                        lane < 2 * GROUP,
                        turns[(1 - k) % 4],
                        jnp.where(lane < 3 * GROUP, turns[(2 - k) % 4], 0.0),
                    ),
                )
                flat[pl.ds(base + 2 * k * quarter + 1, quarter, stride=2), :] = spread


def translate(width, count, ids, table, w_head, w_tail, acc, even, odd, slot_a, slot_b, id_sems):
    rows = acc.shape[0]
    tail = width - LANES
    steps = ids.shape[0] // 2
    flat = table.reshape(2 * table.shape[0], LANES)

    def product(index, source):
        at = pl.ds(pl.multiple_of(index * width, 8), width)
        acc[...] += jnp.dot(
            sources_part(
                source[pl.ds(0, rows, stride=2), :], source[pl.ds(1, rows, stride=2), :]
            ),
            weights(jnp.concatenate([w_head[at, :], w_tail[at, :]], axis=1), tail),
            preferred_element_type=jnp.float32,
        )

    def fetch(unit, slot, k):
        return pltpu.make_async_copy(ids.at[unit, 0], slot, id_sems.at[k])

    def gather(slot, target):
        for r in range(rows):
            target[2 * r : 2 * r + 2, :] = flat[pl.ds(pl.multiple_of(slot[r], 2), 2), :]

    fetch(0, slot_a, 0).start()
    fetch(1, slot_b, 1).start()
    odd[...] = jnp.zeros_like(odd)
    acc[...] = jnp.zeros_like(acc)

    @pl.loop(0, steps)
    def _(j):
        fetch(0, slot_a, 0).wait()
        gather(slot_a, even)
        product(jnp.maximum(2 * j - 1, 0), odd)

        @pl.when(j < steps - 1)
        def _():
            fetch(2 * j + 2, slot_a, 0).start()

        fetch(0, slot_b, 1).wait()
        gather(slot_b, odd)
        product(2 * j, even)

        @pl.when(j < steps - 1)
        def _():
            fetch(2 * j + 3, slot_b, 1).start()

    if 2 * steps == count:
        product(2 * steps - 1, odd)


def reduce_scatter(n, total, inherited, out, outgoing, incoming, send_sems, recv_sems):
    space, me = lax.axis_index("space"), lax.axis_index("sub")
    width, chunk = out.shape
    peers = [lax.rem(me + k, n) for k in range(1, n)]
    barrier = pltpu.get_barrier_semaphore()
    for peer in peers:
        pl.semaphore_signal(
            barrier, inc=1, device_id=(space, peer), device_id_type=pl.DeviceIdType.MESH
        )
    pl.semaphore_wait(barrier, n - 1)
    copies = []
    for k, peer in enumerate(peers):
        outgoing[k] = total[pl.ds(pl.multiple_of(peer * chunk, chunk), chunk), :].T[:width]
        copy = pltpu.make_async_remote_copy(
            src_ref=outgoing.at[k],
            dst_ref=incoming.at[k],
            send_sem=send_sems.at[k],
            recv_sem=recv_sems.at[k],
            device_id=(space, peer),
            device_id_type=pl.DeviceIdType.MESH,
        )
        copy.start()
        copies.append(copy)
    out[...] = inherited[...] + total[pl.ds(pl.multiple_of(me * chunk, chunk), chunk), :].T[:width]
    for k, copy in enumerate(copies):
        copy.wait()
        out[...] += incoming[k]


def local(n_space, n, multipole, inherited, send_rows, sources, operators):
    rows, width = multipole.shape
    count = operators.shape[0]
    slots, gh = send_rows.shape[1:]
    empty_row = rows + slots * gh
    held = count + count % 2
    safe = jnp.where(sources >= 0, 2 * sources, 2 * empty_row)
    safe = jnp.pad(safe, ((0, 0), (0, held - count)), constant_values=2 * empty_row)
    ids = safe.T.reshape(held, 1, rows)
    vmem = pl.BlockSpec(memory_space=pltpu.VMEM)
    smem = pl.BlockSpec(memory_space=pltpu.SMEM)
    chunk = rows // n
    dma = pltpu.SemaphoreType.DMA
    f32 = jnp.float32
    held_rows = -(-held // 8) * 8 * width
    table, w_head, w_tail = pl.pallas_call(
        functools.partial(exchange, (n_space, slots // 2, gh)),
        in_specs=[smem, vmem, pl.BlockSpec(memory_space=pl.ANY)],
        out_specs=[vmem] * 3,
        out_shape=[
            jax.ShapeDtypeStruct((empty_row + 8, 2, LANES), f32),
            jax.ShapeDtypeStruct((held_rows, LANES), f32),
            jax.ShapeDtypeStruct((held_rows, LANES), f32),
        ],
        scratch_shapes=[
            pltpu.VMEM((gh, 2, LANES), f32),
            pltpu.VMEM((slots, gh + gh // 4, LANES), f32),
            pltpu.VMEM((slots, gh + gh // 4, LANES), f32),
            pltpu.VMEM((width, width, count), f32),
            dma((PARTS,)),
            dma((slots,)),
            dma((slots,)),
        ],
        compiler_params=pltpu.CompilerParams(
            collective_id=0, has_side_effects=True, vmem_limit_bytes=36 * 1024 * 1024
        ),
        name="exchange",
    )(send_rows.reshape(-1), multipole.T, operators.transpose(1, 2, 0))
    total = pl.pallas_call(
        functools.partial(translate, width, count),
        in_specs=[vmem] * 4,
        out_specs=vmem,
        out_shape=jax.ShapeDtypeStruct((rows, 2 * LANES), f32),
        scratch_shapes=[
            pltpu.VMEM((2 * rows, LANES), f32),
            pltpu.VMEM((2 * rows, LANES), f32),
            pltpu.SMEM((rows,), jnp.int32),
            pltpu.SMEM((rows,), jnp.int32),
            dma((2,)),
        ],
        compiler_params=pltpu.CompilerParams(vmem_limit_bytes=30 * 1024 * 1024),
        name="translate",
    )(ids, table, w_head, w_tail)
    out = pl.pallas_call(
        functools.partial(reduce_scatter, n),
        in_specs=[vmem] * 2,
        out_specs=vmem,
        out_shape=jax.ShapeDtypeStruct((width, chunk), f32),
        scratch_shapes=[
            pltpu.VMEM((n - 1, width, chunk), f32),
            pltpu.VMEM((n - 1, width, chunk), f32),
            dma((n - 1,)),
            dma((n - 1,)),
        ],
        compiler_params=pltpu.CompilerParams(
            collective_id=1, has_side_effects=True, vmem_limit_bytes=8 * 1024 * 1024
        ),
        name="reduce_scatter",
    )(total, inherited.T)
    return out.T


def solution(mesh):
    return jax.shard_map(
        functools.partial(local, mesh.shape["space"], mesh.shape["sub"]),
        mesh=mesh,
        in_specs=(
            P("space", None),
            P(("space", "sub"), None),
            P("space", None, None),
            P("space", "sub"),
            P("sub", None, None),
        ),
        out_specs=P(("space", "sub"), None),
        check_vma=False,
    )
```

```python
import functools

import jax
import jax.numpy as jnp
from jax import lax
from jax.experimental import pallas as pl
from jax.experimental.pallas import tpu as pltpu
from jax.sharding import PartitionSpec as P

LANES = 128
GROUP = LANES // 4
MESH = pl.DeviceIdType.MESH
PARTS = 4
BLOCKS = 8


def spread_rows(tail):
    pad = jnp.zeros((GROUP - tail.shape[0], tail.shape[1]), jnp.float32)
    end = jnp.zeros((GROUP, tail.shape[1]), jnp.float32)
    return jnp.concatenate([tail, pad, tail, pad, tail, pad, end], axis=0)


def weights(full, tail):
    high = full.astype(jnp.bfloat16).astype(jnp.float32)
    low = full - high
    pad = jnp.zeros((GROUP - tail, full.shape[1]), jnp.float32)
    end = jnp.zeros((GROUP, full.shape[1]), jnp.float32)
    mix = jnp.concatenate([high[LANES:], pad, high[LANES:], pad, low[LANES:], pad, end], axis=0)
    first = high[:LANES].astype(jnp.bfloat16)
    second = low[:LANES].astype(jnp.bfloat16)
    return jnp.concatenate([first, first, second, mix.astype(jnp.bfloat16)], axis=0)


def split(head, rest):
    high = head.astype(jnp.bfloat16).astype(jnp.float32)
    low = (head - high).astype(jnp.bfloat16).astype(jnp.float32)
    rest_high = rest.astype(jnp.bfloat16).astype(jnp.float32)
    rest_low = (rest - rest_high).astype(jnp.bfloat16).astype(jnp.float32)
    lane = lax.broadcasted_iota(jnp.int32, rest.shape, 1)
    second = (lane >= GROUP) & (lane < 2 * GROUP)
    return high, low, jnp.where(second, rest_low, rest_high)


def exchange(
    dims, send_map, block, ops, table, w_head, w_tail, own, picked, stage, land, raw,
    raw_sems, ghost_send, ghost_recv,
):
    n_space, near, gh = dims
    width, rows = block.shape
    count = ops.shape[2]
    tail = width - LANES
    slots = 2 * near
    space, me = lax.axis_index("space"), lax.axis_index("sub")
    offsets = [j + 1 if j < near else near - 1 - j for j in range(slots)]
    flat = table.reshape(4 * table.shape[0], LANES)
    flat_own = own.reshape(2 * rows, LANES)
    flat_picked = picked.reshape(2 * gh, LANES)

    per = width // PARTS
    raw_copies = []
    for k in range(PARTS):
        copy = pltpu.make_async_copy(
            ops.at[pl.ds(k * per, per)], raw.at[pl.ds(k * per, per)], raw_sems.at[k]
        )
        copy.start()
        raw_copies.append(copy)

    barrier = pltpu.get_barrier_semaphore()
    met = 0
    for offset in offsets:
        there = (space + offset >= 0) & (space + offset < n_space)
        met = met + there.astype(jnp.int32)

        @pl.when(there)
        def _():
            pl.semaphore_signal(barrier, inc=1, device_id=(space + offset, me), device_id_type=MESH)

    def widen(start, head, rest):
        for k, part in enumerate(split(head, rest)):
            flat[pl.ds(4 * start + k, head.shape[0], stride=4), :] = part

    flat_own[pl.ds(0, rows, stride=2), :] = block[:LANES, :].T
    flat_own[pl.ds(1, rows, stride=2), :] = spread_rows(block[LANES:, :]).T

    pl.semaphore_wait(barrier, met)

    quarter = gh // 4
    lane = lax.broadcasted_iota(jnp.int32, (quarter, LANES), 1)
    copies = []
    for j, offset in enumerate(offsets):
        there = (space + offset >= 0) & (space + offset < n_space)
        for g in range(gh):
            picked[g] = own[send_map[j * gh + g]]
        stage[j, :gh] = flat_picked[pl.ds(0, gh, stride=2), :]
        q = [flat_picked[pl.ds(2 * k * quarter + 1, quarter, stride=2), :] for k in range(4)]
        stage[j, gh:] = jnp.where(
            lane < GROUP,
            q[0],
            jnp.where(
                lane < 2 * GROUP,
                q[1],
                jnp.where(lane < 3 * GROUP, q[2], pltpu.roll(q[3], 3 * GROUP, 1)),
            ),
        )
        copy = pltpu.make_async_remote_copy(
            src_ref=stage.at[j],
            dst_ref=land.at[j],
            send_sem=ghost_send.at[j],
            recv_sem=ghost_recv.at[j],
            device_id=(jnp.clip(space + offset, 0, n_space - 1), me),
            device_id_type=MESH,
        )
        copies.append(copy)

        @pl.when(there)
        def _():
            copy.start()

    first_free = 4 * (rows + slots * gh)
    flat[first_free:, :] = jnp.zeros((flat.shape[0] - first_free, LANES), jnp.float32)

    @pl.loop(0, rows, step=LANES)
    def _(start):
        at = [pl.ds(2 * start + u, LANES, stride=2) for u in range(2)]
        widen(start, flat_own[at[0], :], flat_own[at[1], :])

    held = w_head.shape[0] // width

    for k in range(PARTS):
        raw_copies[k].wait()

        @pl.loop(k * per, (k + 1) * per, step=2)
        def _(i0):
            for u in range(2):
                i = i0 + u
                slab = raw[i]
                slab = jnp.concatenate(
                    [slab, jnp.zeros((width, LANES - count), jnp.float32)], axis=1
                )
                turned = slab.T
                w_head[pl.ds(i, held, stride=width), :] = turned[:held, :LANES]
                w_tail[pl.ds(i, held, stride=width), :] = jnp.concatenate(
                    [turned[:held, LANES:], jnp.zeros((held, LANES - tail), jnp.float32)], axis=1
                )

    for j, offset in enumerate(offsets):
        there = (space + offset >= 0) & (space + offset < n_space)
        here = (space - offset >= 0) & (space - offset < n_space)

        @pl.when(there)
        def _():
            copies[j].wait_send()

        @pl.when(here)
        def _():
            copies[j].wait_recv()
            base = rows + j * gh
            packed = land[j, gh:]
            turns = [packed] + [pltpu.roll(packed, d * GROUP, 1) for d in range(1, 4)]
            for k in range(4):
                spread = jnp.where(
                    lane < GROUP,
                    turns[(0 - k) % 4],
                    jnp.where(
                        lane < 2 * GROUP,
                        turns[(1 - k) % 4],
                        jnp.where(lane < 3 * GROUP, turns[(2 - k) % 4], 0.0),
                    ),
                )
                widen(base + k * quarter, land[j, pl.ds(k * quarter, quarter)], spread)


def translate(width, count, ids, table, w_head, w_tail, acc, even, odd, slot_a, slot_b, id_sems):
    rows = acc.shape[0]
    tail = width - LANES
    steps = ids.shape[0] // 2
    flat = table.reshape(4 * table.shape[0], LANES)
    slots = (slot_a, slot_b)
    part = rows // BLOCKS

    def product(index, source):
        at = pl.ds(pl.multiple_of(index * width, 8), width)
        held = weights(jnp.concatenate([w_head[at, :], w_tail[at, :]], axis=1), tail)
        for u in range(BLOCKS):
            high, low, mix = [
                source[pl.ds(4 * u * part + k, part, stride=4), :].astype(jnp.bfloat16)
                for k in range(3)
            ]
            acc[u * part : (u + 1) * part, :] += jnp.dot(
                jnp.concatenate([high, low, high, mix], axis=1),
                held,
                preferred_element_type=jnp.float32,
            )

    order = [
        (2 * b + u) * part + v for b in range(BLOCKS // 2) for v in range(part) for u in range(2)
    ]

    def fetch(pair, k):
        return pltpu.make_async_copy(ids.at[pair, 0], slots[k], id_sems.at[k])

    def gather(slot, first, target):
        for r in order:
            target[4 * r : 4 * r + 4, :] = flat[pl.ds(pl.multiple_of(slot[first + r], 4), 4), :]

    fetch(0, 0).start()
    fetch(1, 1).start()
    acc[...] = jnp.zeros_like(acc)

    @pl.loop(0, steps)
    def _(j):
        for k in range(2):
            pair = 2 * j + k
            fetch(0, k).wait()
            gather(slots[k], 0, even)
            product(2 * pair, even)
            gather(slots[k], rows, odd)
            product(2 * pair + 1, odd)

            @pl.when(j < steps - 1)
            def _():
                fetch(pair + 2, k).start()


def reduce_scatter(n, total, inherited, out, outgoing, incoming, send_sems, recv_sems):
    space, me = lax.axis_index("space"), lax.axis_index("sub")
    width, chunk = out.shape
    peers = [lax.rem(me + k, n) for k in range(1, n)]
    barrier = pltpu.get_barrier_semaphore()
    for peer in peers:
        pl.semaphore_signal(
            barrier, inc=1, device_id=(space, peer), device_id_type=pl.DeviceIdType.MESH
        )
    pl.semaphore_wait(barrier, n - 1)
    copies = []
    for k, peer in enumerate(peers):
        outgoing[k] = total[pl.ds(pl.multiple_of(peer * chunk, chunk), chunk), :].T[:width]
        copy = pltpu.make_async_remote_copy(
            src_ref=outgoing.at[k],
            dst_ref=incoming.at[k],
            send_sem=send_sems.at[k],
            recv_sem=recv_sems.at[k],
            device_id=(space, peer),
            device_id_type=pl.DeviceIdType.MESH,
        )
        copy.start()
        copies.append(copy)
    out[...] = inherited[...] + total[pl.ds(pl.multiple_of(me * chunk, chunk), chunk), :].T[:width]
    for k, copy in enumerate(copies):
        copy.wait()
        out[...] += incoming[k]


def local(n_space, n, multipole, inherited, send_rows, sources, operators):
    rows, width = multipole.shape
    count = operators.shape[0]
    slots, gh = send_rows.shape[1:]
    empty_row = rows + slots * gh
    held = -(-count // 4) * 4
    safe = jnp.where(sources >= 0, 4 * sources, 4 * empty_row)
    safe = jnp.pad(safe, ((0, 0), (0, held - count)), constant_values=4 * empty_row)
    ids = safe.T.reshape(held // 2, 1, 2 * rows)
    vmem = pl.BlockSpec(memory_space=pltpu.VMEM)
    smem = pl.BlockSpec(memory_space=pltpu.SMEM)
    chunk = rows // n
    dma = pltpu.SemaphoreType.DMA
    f32 = jnp.float32
    held_rows = -(-held // 8) * 8 * width
    table, w_head, w_tail = pl.pallas_call(
        functools.partial(exchange, (n_space, slots // 2, gh)),
        in_specs=[smem, vmem, pl.BlockSpec(memory_space=pl.ANY)],
        out_specs=[vmem] * 3,
        out_shape=[
            jax.ShapeDtypeStruct((empty_row + 8, 4, LANES), f32),
            jax.ShapeDtypeStruct((held_rows, LANES), f32),
            jax.ShapeDtypeStruct((held_rows, LANES), f32),
        ],
        scratch_shapes=[
            pltpu.VMEM((rows, 2, LANES), f32),
            pltpu.VMEM((gh, 2, LANES), f32),
            pltpu.VMEM((slots, gh + gh // 4, LANES), f32),
            pltpu.VMEM((slots, gh + gh // 4, LANES), f32),
            pltpu.VMEM((width, width, count), f32),
            dma((PARTS,)),
            dma((slots,)),
            dma((slots,)),
        ],
        compiler_params=pltpu.CompilerParams(
            collective_id=0, has_side_effects=True, vmem_limit_bytes=20 * 1024 * 1024
        ),
        name="exchange",
    )(send_rows.reshape(-1), multipole.T, operators.transpose(1, 2, 0))
    total = pl.pallas_call(
        functools.partial(translate, width, count),
        in_specs=[vmem] * 4,
        out_specs=vmem,
        out_shape=jax.ShapeDtypeStruct((rows, 2 * LANES), f32),
        scratch_shapes=[
            pltpu.VMEM((4 * rows, LANES), f32),
            pltpu.VMEM((4 * rows, LANES), f32),
            pltpu.SMEM((2 * rows,), jnp.int32),
            pltpu.SMEM((2 * rows,), jnp.int32),
            dma((2,)),
        ],
        compiler_params=pltpu.CompilerParams(vmem_limit_bytes=16 * 1024 * 1024),
        name="translate",
    )(ids, table, w_head, w_tail)
    out = pl.pallas_call(
        functools.partial(reduce_scatter, n),
        in_specs=[vmem] * 2,
        out_specs=vmem,
        out_shape=jax.ShapeDtypeStruct((width, chunk), f32),
        scratch_shapes=[
            pltpu.VMEM((n - 1, width, chunk), f32),
            pltpu.VMEM((n - 1, width, chunk), f32),
            dma((n - 1,)),
            dma((n - 1,)),
        ],
        compiler_params=pltpu.CompilerParams(
            collective_id=1, has_side_effects=True, vmem_limit_bytes=8 * 1024 * 1024
        ),
        name="reduce_scatter",
    )(total, inherited.T)
    return out.T


def solution(mesh):
    return jax.shard_map(
        functools.partial(local, mesh.shape["space"], mesh.shape["sub"]),
        mesh=mesh,
        in_specs=(
            P("space", None),
            P(("space", "sub"), None),
            P("space", None, None),
            P("space", "sub"),
            P("sub", None, None),
        ),
        out_specs=P(("space", "sub"), None),
        check_vma=False,
    )
```

```python
import functools

import jax
import jax.numpy as jnp
from jax import lax
from jax.experimental import pallas as pl
from jax.experimental.pallas import tpu as pltpu
from jax.sharding import PartitionSpec as P

LANES = 128
GROUP = LANES // 4
MESH = pl.DeviceIdType.MESH
PARTS = 4
BLOCKS = 4


def spread_rows(tail):
    pad = jnp.zeros((GROUP - tail.shape[0], tail.shape[1]), jnp.float32)
    end = jnp.zeros((GROUP, tail.shape[1]), jnp.float32)
    return jnp.concatenate([tail, pad, tail, pad, tail, pad, end], axis=0)


def weights(full, tail):
    high = full.astype(jnp.bfloat16).astype(jnp.float32)
    low = full - high
    pad = jnp.zeros((GROUP - tail, full.shape[1]), jnp.float32)
    end = jnp.zeros((GROUP, full.shape[1]), jnp.float32)
    mix = jnp.concatenate([high[LANES:], pad, high[LANES:], pad, low[LANES:], pad, end], axis=0)
    first = high[:LANES].astype(jnp.bfloat16)
    second = low[:LANES].astype(jnp.bfloat16)
    return jnp.concatenate([first, first, second, mix.astype(jnp.bfloat16)], axis=0)


def split(head, rest):
    high = head.astype(jnp.bfloat16).astype(jnp.float32)
    low = (head - high).astype(jnp.bfloat16).astype(jnp.float32)
    rest_high = rest.astype(jnp.bfloat16).astype(jnp.float32)
    rest_low = (rest - rest_high).astype(jnp.bfloat16).astype(jnp.float32)
    lane = lax.broadcasted_iota(jnp.int32, rest.shape, 1)
    second = (lane >= GROUP) & (lane < 2 * GROUP)
    return high, low, jnp.where(second, rest_low, rest_high)


def exchange(
    dims, send_map, block, ops, table, w_head, w_tail, own, picked, stage, land, raw,
    raw_sems, ghost_send, ghost_recv, pass_send, pass_recv,
):
    n_space, near, gh = dims
    width, rows = block.shape
    count = ops.shape[2]
    tail = width - LANES
    slots = 2 * near
    space, me = lax.axis_index("space"), lax.axis_index("sub")
    offsets = [j + 1 if j < near else near - 1 - j for j in range(slots)]
    flat = table.reshape(4 * table.shape[0], LANES)
    flat_own = own.reshape(2 * rows, LANES)
    flat_picked = picked.reshape(gh, LANES)

    per = width // PARTS
    raw_copies = []
    for k in range(PARTS):
        copy = pltpu.make_async_copy(
            ops.at[pl.ds(k * per, per)], raw.at[pl.ds(k * per, per)], raw_sems.at[k]
        )
        copy.start()
        raw_copies.append(copy)

    mine = lax.rem(me, 2)
    partner = me + 1 - 2 * mine
    share = gh // 2
    start = mine * share

    barrier = pltpu.get_barrier_semaphore()
    met = 1
    pl.semaphore_signal(barrier, inc=1, device_id=(space, partner), device_id_type=MESH)
    for offset in offsets:
        there = (space + offset >= 0) & (space + offset < n_space)
        met = met + there.astype(jnp.int32)

        @pl.when(there)
        def _():
            pl.semaphore_signal(barrier, inc=1, device_id=(space + offset, me), device_id_type=MESH)

    def widen(start, head, rest):
        for k, part in enumerate(split(head, rest)):
            flat[pl.ds(4 * start + k, head.shape[0], stride=4), :] = part

    flat_own[pl.ds(0, rows, stride=2), :] = block[:LANES, :].T
    flat_own[pl.ds(1, rows, stride=2), :] = spread_rows(block[LANES:, :]).T

    pl.semaphore_wait(barrier, met)

    quarter = share // 4
    lane = lax.broadcasted_iota(jnp.int32, (quarter, LANES), 1)
    copies = []
    for j, offset in enumerate(offsets):
        there = (space + offset >= 0) & (space + offset < n_space)
        for g in range(share):
            picked[g] = own[send_map[j * gh + start + g]]
        stage[j, :share] = flat_picked[pl.ds(0, share, stride=2), :]
        q = [flat_picked[pl.ds(2 * k * quarter + 1, quarter, stride=2), :] for k in range(4)]
        stage[j, share:] = jnp.where(
            lane < GROUP,
            q[0],
            jnp.where(
                lane < 2 * GROUP,
                q[1],
                jnp.where(lane < 3 * GROUP, q[2], pltpu.roll(q[3], 3 * GROUP, 1)),
            ),
        )
        copy = pltpu.make_async_remote_copy(
            src_ref=stage.at[j],
            dst_ref=land.at[j, mine],
            send_sem=ghost_send.at[j],
            recv_sem=ghost_recv.at[j],
            device_id=(jnp.clip(space + offset, 0, n_space - 1), me),
            device_id_type=MESH,
        )
        copies.append(copy)

        @pl.when(there)
        def _():
            copy.start()

    first_free = 4 * (rows + slots * gh)
    flat[first_free:, :] = jnp.zeros((flat.shape[0] - first_free, LANES), jnp.float32)

    @pl.loop(0, rows, step=LANES)
    def _(first):
        at = [pl.ds(2 * first + u, LANES, stride=2) for u in range(2)]
        widen(first, flat_own[at[0], :], flat_own[at[1], :])

    held = w_head.shape[0] // width

    def turn(k):
        raw_copies[k].wait()

        @pl.loop(k * per, (k + 1) * per, step=2)
        def _(i0):
            for u in range(2):
                i = i0 + u
                slab = raw[i]
                slab = jnp.concatenate(
                    [slab, jnp.zeros((width, LANES - count), jnp.float32)], axis=1
                )
                turned = slab.T
                w_head[pl.ds(i, held, stride=width), :] = turned[:held, :LANES]
                w_tail[pl.ds(i, held, stride=width), :] = jnp.concatenate(
                    [turned[:held, LANES:], jnp.zeros((held, LANES - tail), jnp.float32)], axis=1
                )

    def ghost_rows(j, which):
        base = rows + j * gh + which * share
        packed = land[j, which, share:]
        turns = [packed] + [pltpu.roll(packed, d * GROUP, 1) for d in range(1, 4)]
        for k in range(4):
            spread = jnp.where(
                lane < GROUP,
                turns[(0 - k) % 4],
                jnp.where(
                    lane < 2 * GROUP,
                    turns[(1 - k) % 4],
                    jnp.where(lane < 3 * GROUP, turns[(2 - k) % 4], 0.0),
                ),
            )
            widen(base + k * quarter, land[j, which, pl.ds(k * quarter, quarter)], spread)

    for k in range(PARTS - 1):
        turn(k)

    passes = []
    for j, offset in enumerate(offsets):
        here = (space - offset >= 0) & (space - offset < n_space)
        copy = pltpu.make_async_remote_copy(
            src_ref=land.at[j, mine],
            dst_ref=land.at[j, mine],
            send_sem=pass_send.at[j],
            recv_sem=pass_recv.at[j],
            device_id=(space, partner),
            device_id_type=MESH,
        )
        passes.append(copy)

        @pl.when(here)
        def _():
            copies[j].wait_recv()
            copy.start()

    turn(PARTS - 1)

    for j, offset in enumerate(offsets):
        there = (space + offset >= 0) & (space + offset < n_space)
        here = (space - offset >= 0) & (space - offset < n_space)

        @pl.when(there)
        def _():
            copies[j].wait_send()

        @pl.when(here)
        def _():
            ghost_rows(j, mine)

    for j, offset in enumerate(offsets):
        here = (space - offset >= 0) & (space - offset < n_space)

        @pl.when(here)
        def _():
            passes[j].wait()
            ghost_rows(j, 1 - mine)


def translate(width, count, ids, table, w_head, w_tail, acc, even, odd, slot_a, slot_b, id_sems):
    rows = acc.shape[0]
    tail = width - LANES
    steps = ids.shape[0] // 2
    flat = table.reshape(4 * table.shape[0], LANES)
    slots = (slot_a, slot_b)
    part = rows // BLOCKS

    def product(index, source):
        at = pl.ds(pl.multiple_of(index * width, 8), width)
        held = weights(jnp.concatenate([w_head[at, :], w_tail[at, :]], axis=1), tail)
        for u in range(BLOCKS):
            high, low, mix = [
                source[pl.ds(4 * u * part + k, part, stride=4), :].astype(jnp.bfloat16)
                for k in range(3)
            ]
            acc[u * part : (u + 1) * part, :] += jnp.dot(
                jnp.concatenate([high, low, high, mix], axis=1),
                held,
                preferred_element_type=jnp.float32,
            )

    order = [
        (2 * b + u) * part + v for b in range(BLOCKS // 2) for v in range(part) for u in range(2)
    ]

    def fetch(pair, k):
        return pltpu.make_async_copy(ids.at[pair, 0], slots[k], id_sems.at[k])

    def gather(slot, first, target):
        for r in order:
            target[4 * r : 4 * r + 4, :] = flat[pl.ds(pl.multiple_of(slot[first + r], 4), 4), :]

    fetch(0, 0).start()
    fetch(1, 1).start()
    acc[...] = jnp.zeros_like(acc)

    @pl.loop(0, steps)
    def _(j):
        for k in range(2):
            pair = 2 * j + k
            fetch(0, k).wait()
            gather(slots[k], 0, even)
            product(2 * pair, even)
            gather(slots[k], rows, odd)
            product(2 * pair + 1, odd)

            @pl.when(j < steps - 1)
            def _():
                fetch(pair + 2, k).start()


def reduce_scatter(n, total, inherited, out, outgoing, incoming, send_sems, recv_sems):
    space, me = lax.axis_index("space"), lax.axis_index("sub")
    width, chunk = out.shape
    peers = [lax.rem(me + k, n) for k in range(1, n)]
    barrier = pltpu.get_barrier_semaphore()
    for peer in peers:
        pl.semaphore_signal(
            barrier, inc=1, device_id=(space, peer), device_id_type=pl.DeviceIdType.MESH
        )
    pl.semaphore_wait(barrier, n - 1)
    copies = []
    for k, peer in enumerate(peers):
        outgoing[k] = total[pl.ds(pl.multiple_of(peer * chunk, chunk), chunk), :].T[:width]
        copy = pltpu.make_async_remote_copy(
            src_ref=outgoing.at[k],
            dst_ref=incoming.at[k],
            send_sem=send_sems.at[k],
            recv_sem=recv_sems.at[k],
            device_id=(space, peer),
            device_id_type=pl.DeviceIdType.MESH,
        )
        copy.start()
        copies.append(copy)
    out[...] = inherited[...] + total[pl.ds(pl.multiple_of(me * chunk, chunk), chunk), :].T[:width]
    for k, copy in enumerate(copies):
        copy.wait()
        out[...] += incoming[k]


def local(n_space, n, multipole, inherited, send_rows, sources, operators):
    rows, width = multipole.shape
    count = operators.shape[0]
    slots, gh = send_rows.shape[1:]
    empty_row = rows + slots * gh
    held = -(-count // 4) * 4
    safe = jnp.where(sources >= 0, 4 * sources, 4 * empty_row)
    safe = jnp.pad(safe, ((0, 0), (0, held - count)), constant_values=4 * empty_row)
    ids = safe.T.reshape(held // 2, 1, 2 * rows)
    vmem = pl.BlockSpec(memory_space=pltpu.VMEM)
    smem = pl.BlockSpec(memory_space=pltpu.SMEM)
    chunk = rows // n
    dma = pltpu.SemaphoreType.DMA
    f32 = jnp.float32
    held_rows = -(-held // 8) * 8 * width
    table, w_head, w_tail = pl.pallas_call(
        functools.partial(exchange, (n_space, slots // 2, gh)),
        in_specs=[smem, vmem, pl.BlockSpec(memory_space=pl.ANY)],
        out_specs=[vmem] * 3,
        out_shape=[
            jax.ShapeDtypeStruct((empty_row + 8, 4, LANES), f32),
            jax.ShapeDtypeStruct((held_rows, LANES), f32),
            jax.ShapeDtypeStruct((held_rows, LANES), f32),
        ],
        scratch_shapes=[
            pltpu.VMEM((rows, 2, LANES), f32),
            pltpu.VMEM((gh // 2, 2, LANES), f32),
            pltpu.VMEM((slots, gh // 2 + gh // 8, LANES), f32),
            pltpu.VMEM((slots, 2, gh // 2 + gh // 8, LANES), f32),
            pltpu.VMEM((width, width, count), f32),
            dma((PARTS,)),
            dma((slots,)),
            dma((slots,)),
            dma((slots,)),
            dma((slots,)),
        ],
        compiler_params=pltpu.CompilerParams(
            collective_id=0, has_side_effects=True, vmem_limit_bytes=28 * 1024 * 1024
        ),
        name="exchange",
    )(send_rows.reshape(-1), multipole.T, operators.transpose(1, 2, 0))
    total = pl.pallas_call(
        functools.partial(translate, width, count),
        in_specs=[vmem] * 4,
        out_specs=vmem,
        out_shape=jax.ShapeDtypeStruct((rows, 2 * LANES), f32),
        scratch_shapes=[
            pltpu.VMEM((4 * rows, LANES), f32),
            pltpu.VMEM((4 * rows, LANES), f32),
            pltpu.SMEM((2 * rows,), jnp.int32),
            pltpu.SMEM((2 * rows,), jnp.int32),
            dma((2,)),
        ],
        compiler_params=pltpu.CompilerParams(vmem_limit_bytes=16 * 1024 * 1024),
        name="translate",
    )(ids, table, w_head, w_tail)
    out = pl.pallas_call(
        functools.partial(reduce_scatter, n),
        in_specs=[vmem] * 2,
        out_specs=vmem,
        out_shape=jax.ShapeDtypeStruct((width, chunk), f32),
        scratch_shapes=[
            pltpu.VMEM((n - 1, width, chunk), f32),
            pltpu.VMEM((n - 1, width, chunk), f32),
            dma((n - 1,)),
            dma((n - 1,)),
        ],
        compiler_params=pltpu.CompilerParams(
            collective_id=1, has_side_effects=True, vmem_limit_bytes=8 * 1024 * 1024
        ),
        name="reduce_scatter",
    )(total, inherited.T)
    return out.T


def solution(mesh):
    return jax.shard_map(
        functools.partial(local, mesh.shape["space"], mesh.shape["sub"]),
        mesh=mesh,
        in_specs=(
            P("space", None),
            P(("space", "sub"), None),
            P("space", None, None),
            P("space", "sub"),
            P("sub", None, None),
        ),
        out_specs=P(("space", "sub"), None),
        check_vma=False,
    )
```

```python
import functools

import jax
import jax.numpy as jnp
from jax import lax
from jax.experimental import pallas as pl
from jax.experimental.pallas import tpu as pltpu
from jax.sharding import PartitionSpec as P

LANES = 128
GROUP = LANES // 4
MESH = pl.DeviceIdType.MESH
PARTS = 4
BLOCKS = 4
EACH = 4


def odd_stride(width):
    return width + 1 - width % 2


def spread_rows(tail):
    pad = jnp.zeros((GROUP - tail.shape[0], tail.shape[1]), jnp.float32)
    end = jnp.zeros((GROUP, tail.shape[1]), jnp.float32)
    return jnp.concatenate([tail, pad, tail, pad, tail, pad, end], axis=0)


def weights(full, tail):
    high = full.astype(jnp.bfloat16).astype(jnp.float32)
    low = full - high
    pad = jnp.zeros((GROUP - tail, full.shape[1]), jnp.float32)
    end = jnp.zeros((GROUP, full.shape[1]), jnp.float32)
    mix = jnp.concatenate([high[LANES:], pad, high[LANES:], pad, low[LANES:], pad, end], axis=0)
    first = high[:LANES].astype(jnp.bfloat16)
    second = low[:LANES].astype(jnp.bfloat16)
    return jnp.concatenate([first, first, second, mix.astype(jnp.bfloat16)], axis=0)


def split(head, rest):
    high = head.astype(jnp.bfloat16).astype(jnp.float32)
    low = (head - high).astype(jnp.bfloat16).astype(jnp.float32)
    rest_high = rest.astype(jnp.bfloat16).astype(jnp.float32)
    rest_low = (rest - rest_high).astype(jnp.bfloat16).astype(jnp.float32)
    lane = lax.broadcasted_iota(jnp.int32, rest.shape, 1)
    second = (lane >= GROUP) & (lane < 2 * GROUP)
    return high, low, jnp.where(second, rest_low, rest_high)


def exchange(
    dims, send_map, block, ops, table, w_head, w_tail, own, picked, stage, land, raw,
    raw_sems, ghost_send, ghost_recv, pass_send, pass_recv,
):
    n_space, near, gh = dims
    width, rows = block.shape
    count = ops.shape[2]
    tail = width - LANES
    slots = 2 * near
    space, me = lax.axis_index("space"), lax.axis_index("sub")
    offsets = [j + 1 if j < near else near - 1 - j for j in range(slots)]
    flat = table.reshape(4 * table.shape[0], LANES)
    flat_own = own.reshape(2 * rows, LANES)
    flat_picked = picked.reshape(gh, LANES)

    per = width // PARTS
    raw_copies = []
    for k in range(PARTS):
        copy = pltpu.make_async_copy(
            ops.at[pl.ds(k * per, per)], raw.at[pl.ds(k * per, per)], raw_sems.at[k]
        )
        copy.start()
        raw_copies.append(copy)

    mine = lax.rem(me, 2)
    partner = me + 1 - 2 * mine
    share = gh // 2
    start = mine * share

    barrier = pltpu.get_barrier_semaphore()
    met = 1
    pl.semaphore_signal(barrier, inc=1, device_id=(space, partner), device_id_type=MESH)
    for offset in offsets:
        there = (space + offset >= 0) & (space + offset < n_space)
        met = met + there.astype(jnp.int32)

        @pl.when(there)
        def _():
            pl.semaphore_signal(barrier, inc=1, device_id=(space + offset, me), device_id_type=MESH)

    def widen(start, head, rest):
        for k, part in enumerate(split(head, rest)):
            flat[pl.ds(4 * start + k, head.shape[0], stride=4), :] = part

    flat_own[pl.ds(0, rows, stride=2), :] = block[:LANES, :].T
    flat_own[pl.ds(1, rows, stride=2), :] = spread_rows(block[LANES:, :]).T

    pl.semaphore_wait(barrier, met)

    quarter = share // 4
    lane = lax.broadcasted_iota(jnp.int32, (quarter, LANES), 1)
    copies = []
    for j, offset in enumerate(offsets):
        there = (space + offset >= 0) & (space + offset < n_space)
        for g in range(share):
            picked[g] = own[send_map[j * gh + start + g]]
        stage[j, :share] = flat_picked[pl.ds(0, share, stride=2), :]
        q = [flat_picked[pl.ds(2 * k * quarter + 1, quarter, stride=2), :] for k in range(4)]
        stage[j, share:] = jnp.where(
            lane < GROUP,
            q[0],
            jnp.where(
                lane < 2 * GROUP,
                q[1],
                jnp.where(lane < 3 * GROUP, q[2], pltpu.roll(q[3], 3 * GROUP, 1)),
            ),
        )
        copy = pltpu.make_async_remote_copy(
            src_ref=stage.at[j],
            dst_ref=land.at[j, mine],
            send_sem=ghost_send.at[j],
            recv_sem=ghost_recv.at[j],
            device_id=(jnp.clip(space + offset, 0, n_space - 1), me),
            device_id_type=MESH,
        )
        copies.append(copy)

        @pl.when(there)
        def _():
            copy.start()

    first_free = 4 * (rows + slots * gh)
    flat[first_free:, :] = jnp.zeros((flat.shape[0] - first_free, LANES), jnp.float32)

    @pl.loop(0, rows, step=LANES)
    def _(first):
        at = [pl.ds(2 * first + u, LANES, stride=2) for u in range(2)]
        widen(first, flat_own[at[0], :], flat_own[at[1], :])

    stride = odd_stride(width)
    held = w_head.shape[0] // stride

    def turn(k):
        raw_copies[k].wait()

        @pl.loop(k * per, (k + 1) * per, step=2)
        def _(i0):
            for u in range(2):
                i = i0 + u
                slab = raw[i]
                slab = jnp.concatenate(
                    [slab, jnp.zeros((width, LANES - count), jnp.float32)], axis=1
                )
                turned = slab.T
                w_head[pl.ds(i, held, stride=stride), :] = turned[:held, :LANES]
                w_tail[pl.ds(i, held, stride=stride), :] = jnp.concatenate(
                    [turned[:held, LANES:], jnp.zeros((held, LANES - tail), jnp.float32)], axis=1
                )

    def ghost_rows(j, which):
        base = rows + j * gh + which * share
        packed = land[j, which, share:]
        turns = [packed] + [pltpu.roll(packed, d * GROUP, 1) for d in range(1, 4)]
        for k in range(4):
            spread = jnp.where(
                lane < GROUP,
                turns[(0 - k) % 4],
                jnp.where(
                    lane < 2 * GROUP,
                    turns[(1 - k) % 4],
                    jnp.where(lane < 3 * GROUP, turns[(2 - k) % 4], 0.0),
                ),
            )
            widen(base + k * quarter, land[j, which, pl.ds(k * quarter, quarter)], spread)

    for k in range(PARTS - 1):
        turn(k)

    passes = []
    for j, offset in enumerate(offsets):
        here = (space - offset >= 0) & (space - offset < n_space)
        copy = pltpu.make_async_remote_copy(
            src_ref=land.at[j, mine],
            dst_ref=land.at[j, mine],
            send_sem=pass_send.at[j],
            recv_sem=pass_recv.at[j],
            device_id=(space, partner),
            device_id_type=MESH,
        )
        passes.append(copy)

        @pl.when(here)
        def _():
            copies[j].wait_recv()
            copy.start()

    turn(PARTS - 1)

    for j, offset in enumerate(offsets):
        there = (space + offset >= 0) & (space + offset < n_space)
        here = (space - offset >= 0) & (space - offset < n_space)

        @pl.when(there)
        def _():
            copies[j].wait_send()

        @pl.when(here)
        def _():
            ghost_rows(j, mine)

    for j, offset in enumerate(offsets):
        here = (space - offset >= 0) & (space - offset < n_space)

        @pl.when(here)
        def _():
            passes[j].wait()
            ghost_rows(j, 1 - mine)


def translate(width, count, ids, table, w_head, w_tail, acc, even, odd, slot_a, slot_b, id_sems):
    rows = acc.shape[0]
    tail = width - LANES
    steps = ids.shape[0] // 2
    each = ids.shape[2] // rows
    flat = table.reshape(4 * table.shape[0], LANES)
    slots = (slot_a, slot_b)
    part = rows // BLOCKS

    def product(index, source):
        at = pl.ds(index * odd_stride(width), width)
        held = weights(jnp.concatenate([w_head[at, :], w_tail[at, :]], axis=1), tail)
        for u in range(BLOCKS):
            high, low, mix = [
                source[pl.ds(4 * u * part + k, part, stride=4), :].astype(jnp.bfloat16)
                for k in range(3)
            ]
            acc[u * part : (u + 1) * part, :] += jnp.dot(
                jnp.concatenate([high, low, high, mix], axis=1),
                held,
                preferred_element_type=jnp.float32,
            )

    order = [
        (2 * b + u) * part + v for b in range(BLOCKS // 2) for v in range(part) for u in range(2)
    ]

    def fetch(pair, k):
        return pltpu.make_async_copy(ids.at[pair, 0], slots[k], id_sems.at[k])

    def gather(slot, first, target):
        for r in range(rows):
            target[4 * r : 4 * r + 4, :] = flat[pl.ds(pl.multiple_of(slot[first + r], 4), 4), :]

    fetch(0, 0).start()
    fetch(1, 1).start()
    acc[...] = jnp.zeros_like(acc)

    @pl.loop(0, steps)
    def _(j):
        for k in range(2):
            pair = 2 * j + k
            fetch(0, k).wait()
            for u in range(each):
                gather(slots[k], u * rows, (even, odd)[u % 2])
                product(each * pair + u, (even, odd)[u % 2])

            @pl.when(j < steps - 1)
            def _():
                fetch(pair + 2, k).start()


def reduce_scatter(n, total, inherited, out, outgoing, incoming, send_sems, recv_sems):
    space, me = lax.axis_index("space"), lax.axis_index("sub")
    width, chunk = out.shape
    peers = [lax.rem(me + k, n) for k in range(1, n)]
    barrier = pltpu.get_barrier_semaphore()
    for peer in peers:
        pl.semaphore_signal(
            barrier, inc=1, device_id=(space, peer), device_id_type=pl.DeviceIdType.MESH
        )
    pl.semaphore_wait(barrier, n - 1)
    copies = []
    for k, peer in enumerate(peers):
        outgoing[k] = total[pl.ds(pl.multiple_of(peer * chunk, chunk), chunk), :].T[:width]
        copy = pltpu.make_async_remote_copy(
            src_ref=outgoing.at[k],
            dst_ref=incoming.at[k],
            send_sem=send_sems.at[k],
            recv_sem=recv_sems.at[k],
            device_id=(space, peer),
            device_id_type=pl.DeviceIdType.MESH,
        )
        copy.start()
        copies.append(copy)
    out[...] = inherited[...] + total[pl.ds(pl.multiple_of(me * chunk, chunk), chunk), :].T[:width]
    for k, copy in enumerate(copies):
        copy.wait()
        out[...] += incoming[k]


def local(n_space, n, multipole, inherited, send_rows, sources, operators):
    rows, width = multipole.shape
    count = operators.shape[0]
    slots, gh = send_rows.shape[1:]
    empty_row = rows + slots * gh
    held = -(-count // (2 * EACH)) * 2 * EACH
    safe = jnp.where(sources >= 0, 4 * sources, 4 * empty_row)
    safe = jnp.pad(safe, ((0, 0), (0, held - count)), constant_values=4 * empty_row)
    ids = safe.T.reshape(held // EACH, 1, EACH * rows)
    vmem = pl.BlockSpec(memory_space=pltpu.VMEM)
    smem = pl.BlockSpec(memory_space=pltpu.SMEM)
    chunk = rows // n
    dma = pltpu.SemaphoreType.DMA
    f32 = jnp.float32
    held_rows = -(-held // 8) * 8 * odd_stride(width)
    table, w_head, w_tail = pl.pallas_call(
        functools.partial(exchange, (n_space, slots // 2, gh)),
        in_specs=[smem, vmem, pl.BlockSpec(memory_space=pl.ANY)],
        out_specs=[vmem] * 3,
        out_shape=[
            jax.ShapeDtypeStruct((empty_row + 8, 4, LANES), f32),
            jax.ShapeDtypeStruct((held_rows, LANES), f32),
            jax.ShapeDtypeStruct((held_rows, LANES), f32),
        ],
        scratch_shapes=[
            pltpu.VMEM((rows, 2, LANES), f32),
            pltpu.VMEM((gh // 2, 2, LANES), f32),
            pltpu.VMEM((slots, gh // 2 + gh // 8, LANES), f32),
            pltpu.VMEM((slots, 2, gh // 2 + gh // 8, LANES), f32),
            pltpu.VMEM((width, width, count), f32),
            dma((PARTS,)),
            dma((slots,)),
            dma((slots,)),
            dma((slots,)),
            dma((slots,)),
        ],
        compiler_params=pltpu.CompilerParams(
            collective_id=0, has_side_effects=True, vmem_limit_bytes=28 * 1024 * 1024
        ),
        name="exchange",
    )(send_rows.reshape(-1), multipole.T, operators.transpose(1, 2, 0))
    total = pl.pallas_call(
        functools.partial(translate, width, count),
        in_specs=[vmem] * 4,
        out_specs=vmem,
        out_shape=jax.ShapeDtypeStruct((rows, 2 * LANES), f32),
        scratch_shapes=[
            pltpu.VMEM((4 * rows, LANES), f32),
            pltpu.VMEM((4 * rows, LANES), f32),
            pltpu.SMEM((EACH * rows,), jnp.int32),
            pltpu.SMEM((EACH * rows,), jnp.int32),
            dma((2,)),
        ],
        compiler_params=pltpu.CompilerParams(vmem_limit_bytes=16 * 1024 * 1024),
        name="translate",
    )(ids, table, w_head, w_tail)
    out = pl.pallas_call(
        functools.partial(reduce_scatter, n),
        in_specs=[vmem] * 2,
        out_specs=vmem,
        out_shape=jax.ShapeDtypeStruct((width, chunk), f32),
        scratch_shapes=[
            pltpu.VMEM((n - 1, width, chunk), f32),
            pltpu.VMEM((n - 1, width, chunk), f32),
            dma((n - 1,)),
            dma((n - 1,)),
        ],
        compiler_params=pltpu.CompilerParams(
            collective_id=1, has_side_effects=True, vmem_limit_bytes=8 * 1024 * 1024
        ),
        name="reduce_scatter",
    )(total, inherited.T)
    return out.T


def solution(mesh):
    return jax.shard_map(
        functools.partial(local, mesh.shape["space"], mesh.shape["sub"]),
        mesh=mesh,
        in_specs=(
            P("space", None),
            P(("space", "sub"), None),
            P("space", None, None),
            P("space", "sub"),
            P("sub", None, None),
        ),
        out_specs=P(("space", "sub"), None),
        check_vma=False,
    )
```

```python
import functools

import jax
import jax.numpy as jnp
from jax import lax
from jax.experimental import pallas as pl
from jax.experimental.pallas import tpu as pltpu
from jax.sharding import PartitionSpec as P

LANES = 128
GROUP = LANES // 4
MESH = pl.DeviceIdType.MESH
PARTS = 4
BLOCKS = 4
EACH = 8


def odd_stride(width):
    return width + 1 - width % 2


def spread_rows(tail):
    pad = jnp.zeros((GROUP - tail.shape[0], tail.shape[1]), jnp.float32)
    end = jnp.zeros((GROUP, tail.shape[1]), jnp.float32)
    return jnp.concatenate([tail, pad, tail, pad, tail, pad, end], axis=0)


def weights(full, tail):
    high = full.astype(jnp.bfloat16).astype(jnp.float32)
    low = full - high
    pad = jnp.zeros((GROUP - tail, full.shape[1]), jnp.float32)
    end = jnp.zeros((GROUP, full.shape[1]), jnp.float32)
    mix = jnp.concatenate([high[LANES:], pad, high[LANES:], pad, low[LANES:], pad, end], axis=0)
    first = high[:LANES].astype(jnp.bfloat16)
    second = low[:LANES].astype(jnp.bfloat16)
    return jnp.concatenate([first, first, second, mix.astype(jnp.bfloat16)], axis=0)


def split(head, rest):
    high = head.astype(jnp.bfloat16).astype(jnp.float32)
    low = (head - high).astype(jnp.bfloat16).astype(jnp.float32)
    rest_high = rest.astype(jnp.bfloat16).astype(jnp.float32)
    rest_low = (rest - rest_high).astype(jnp.bfloat16).astype(jnp.float32)
    lane = lax.broadcasted_iota(jnp.int32, rest.shape, 1)
    second = (lane >= GROUP) & (lane < 2 * GROUP)
    return high, low, jnp.where(second, rest_low, rest_high)


def exchange(
    dims, send_map, block, ops, table, w_head, w_tail, own, picked, stage, land, raw,
    raw_sems, ghost_send, ghost_recv, pass_send, pass_recv,
):
    n_space, near, gh = dims
    width, rows = block.shape
    count = ops.shape[2]
    tail = width - LANES
    slots = 2 * near
    space, me = lax.axis_index("space"), lax.axis_index("sub")
    offsets = [j + 1 if j < near else near - 1 - j for j in range(slots)]
    flat = table.reshape(4 * table.shape[0], LANES)
    flat_own = own.reshape(2 * rows, LANES)
    flat_picked = picked.reshape(gh, LANES)

    per = width // PARTS
    raw_copies = []
    for k in range(PARTS):
        copy = pltpu.make_async_copy(
            ops.at[pl.ds(k * per, per)], raw.at[pl.ds(k * per, per)], raw_sems.at[k]
        )
        copy.start()
        raw_copies.append(copy)

    mine = lax.rem(me, 2)
    partner = me + 1 - 2 * mine
    share = gh // 2
    start = mine * share

    barrier = pltpu.get_barrier_semaphore()
    met = 1
    pl.semaphore_signal(barrier, inc=1, device_id=(space, partner), device_id_type=MESH)
    for offset in offsets:
        there = (space + offset >= 0) & (space + offset < n_space)
        met = met + there.astype(jnp.int32)

        @pl.when(there)
        def _():
            pl.semaphore_signal(barrier, inc=1, device_id=(space + offset, me), device_id_type=MESH)

    def widen(start, head, rest):
        for k, part in enumerate(split(head, rest)):
            flat[pl.ds(4 * start + k, head.shape[0], stride=4), :] = part

    flat_own[pl.ds(0, rows, stride=2), :] = block[:LANES, :].T
    flat_own[pl.ds(1, rows, stride=2), :] = spread_rows(block[LANES:, :]).T

    pl.semaphore_wait(barrier, met)

    quarter = share // 4
    lane = lax.broadcasted_iota(jnp.int32, (quarter, LANES), 1)
    copies = []
    for j, offset in enumerate(offsets):
        there = (space + offset >= 0) & (space + offset < n_space)
        for g in range(share):
            picked[g] = own[send_map[j * gh + start + g]]
        stage[j, :share] = flat_picked[pl.ds(0, share, stride=2), :]
        q = [flat_picked[pl.ds(2 * k * quarter + 1, quarter, stride=2), :] for k in range(4)]
        stage[j, share:] = jnp.where(
            lane < GROUP,
            q[0],
            jnp.where(
                lane < 2 * GROUP,
                q[1],
                jnp.where(lane < 3 * GROUP, q[2], pltpu.roll(q[3], 3 * GROUP, 1)),
            ),
        )
        copy = pltpu.make_async_remote_copy(
            src_ref=stage.at[j],
            dst_ref=land.at[j, mine],
            send_sem=ghost_send.at[j],
            recv_sem=ghost_recv.at[j],
            device_id=(jnp.clip(space + offset, 0, n_space - 1), me),
            device_id_type=MESH,
        )
        copies.append(copy)

        @pl.when(there)
        def _():
            copy.start()

    first_free = 4 * (rows + slots * gh)
    flat[first_free:, :] = jnp.zeros((flat.shape[0] - first_free, LANES), jnp.float32)

    @pl.loop(0, rows, step=LANES)
    def _(first):
        at = [pl.ds(2 * first + u, LANES, stride=2) for u in range(2)]
        widen(first, flat_own[at[0], :], flat_own[at[1], :])

    stride = odd_stride(width)
    held = w_head.shape[0] // stride

    def turn(k):
        raw_copies[k].wait()

        @pl.loop(k * per, (k + 1) * per, step=2)
        def _(i0):
            for u in range(2):
                i = i0 + u
                slab = raw[i]
                slab = jnp.concatenate(
                    [slab, jnp.zeros((width, LANES - count), jnp.float32)], axis=1
                )
                turned = slab.T
                w_head[pl.ds(i, held, stride=stride), :] = turned[:held, :LANES]
                w_tail[pl.ds(i, held, stride=stride), :] = jnp.concatenate(
                    [turned[:held, LANES:], jnp.zeros((held, LANES - tail), jnp.float32)], axis=1
                )

    def ghost_rows(j, which):
        base = rows + j * gh + which * share
        packed = land[j, which, share:]
        turns = [packed] + [pltpu.roll(packed, d * GROUP, 1) for d in range(1, 4)]
        for k in range(4):
            spread = jnp.where(
                lane < GROUP,
                turns[(0 - k) % 4],
                jnp.where(
                    lane < 2 * GROUP,
                    turns[(1 - k) % 4],
                    jnp.where(lane < 3 * GROUP, turns[(2 - k) % 4], 0.0),
                ),
            )
            widen(base + k * quarter, land[j, which, pl.ds(k * quarter, quarter)], spread)

    for k in range(PARTS - 1):
        turn(k)

    passes = []
    for j, offset in enumerate(offsets):
        here = (space - offset >= 0) & (space - offset < n_space)
        copy = pltpu.make_async_remote_copy(
            src_ref=land.at[j, mine],
            dst_ref=land.at[j, mine],
            send_sem=pass_send.at[j],
            recv_sem=pass_recv.at[j],
            device_id=(space, partner),
            device_id_type=MESH,
        )
        passes.append(copy)

        @pl.when(here)
        def _():
            copies[j].wait_recv()
            copy.start()

    turn(PARTS - 1)

    for j, offset in enumerate(offsets):
        there = (space + offset >= 0) & (space + offset < n_space)
        here = (space - offset >= 0) & (space - offset < n_space)

        @pl.when(there)
        def _():
            copies[j].wait_send()

        @pl.when(here)
        def _():
            ghost_rows(j, mine)

    for j, offset in enumerate(offsets):
        here = (space - offset >= 0) & (space - offset < n_space)

        @pl.when(here)
        def _():
            passes[j].wait()
            ghost_rows(j, 1 - mine)


def translate(width, count, ids, table, w_head, w_tail, acc, even, odd, slot_a, slot_b, id_sems):
    rows = acc.shape[0]
    tail = width - LANES
    steps = ids.shape[0] // 2
    each = ids.shape[2] // rows
    flat = table.reshape(4 * table.shape[0], LANES)
    slots = (slot_a, slot_b)
    part = rows // BLOCKS

    def product(index, source):
        at = pl.ds(index * odd_stride(width), width)
        held = weights(jnp.concatenate([w_head[at, :], w_tail[at, :]], axis=1), tail)
        for u in range(BLOCKS):
            high, low, mix = [
                source[pl.ds(4 * u * part + k, part, stride=4), :].astype(jnp.bfloat16)
                for k in range(3)
            ]
            acc[u * part : (u + 1) * part, :] += jnp.dot(
                jnp.concatenate([high, low, high, mix], axis=1),
                held,
                preferred_element_type=jnp.float32,
            )

    order = [
        (2 * b + u) * part + v for b in range(BLOCKS // 2) for v in range(part) for u in range(2)
    ]

    def fetch(pair, k):
        return pltpu.make_async_copy(ids.at[pair, 0], slots[k], id_sems.at[k])

    def gather(slot, first, target):
        for r in range(rows):
            target[4 * r : 4 * r + 4, :] = flat[pl.ds(pl.multiple_of(slot[first + r], 4), 4), :]

    fetch(0, 0).start()
    fetch(1, 1).start()
    acc[...] = jnp.zeros_like(acc)

    @pl.loop(0, steps)
    def _(j):
        for k in range(2):
            pair = 2 * j + k
            fetch(0, k).wait()
            for u in range(each):
                gather(slots[k], u * rows, (even, odd)[u % 2])
                product(each * pair + u, (even, odd)[u % 2])

            @pl.when(j < steps - 1)
            def _():
                fetch(pair + 2, k).start()


def reduce_scatter(
    n, total, inherited, out, outgoing, paired, passing, incoming,
    pair_send, pair_recv, send_sems, recv_sems,
):
    space, me = lax.axis_index("space"), lax.axis_index("sub")
    width, chunk = out.shape
    halves = n // 2
    mine, my_half = lax.rem(me, 2), me // 2
    partner = me + 1 - 2 * mine
    others = [lax.rem(my_half + k, halves) for k in range(1, halves)]
    barrier = pltpu.get_barrier_semaphore()
    for peer in [partner] + [2 * q + mine for q in others]:
        pl.semaphore_signal(
            barrier, inc=1, device_id=(space, peer), device_id_type=pl.DeviceIdType.MESH
        )
    pl.semaphore_wait(barrier, halves)

    def piece(owner):
        return total[pl.ds(pl.multiple_of(owner * chunk, chunk), chunk), :].T[:width]

    def copy_to(peer, src, dst, send_sem, recv_sem):
        copy = pltpu.make_async_remote_copy(
            src_ref=src,
            dst_ref=dst,
            send_sem=send_sem,
            recv_sem=recv_sem,
            device_id=(space, peer),
            device_id_type=pl.DeviceIdType.MESH,
        )
        copy.start()
        return copy

    pairs = []
    for t, q in enumerate(others + [my_half]):
        outgoing[t] = piece(2 * q + 1 - mine)
        pairs.append(
            copy_to(partner, outgoing.at[t], paired.at[t], pair_send.at[t], pair_recv.at[t])
        )
    for t, q in enumerate(others):
        passing[t] = piece(2 * q + mine)
    out[...] = inherited[...] + piece(me)
    copies = []
    for t, q in enumerate(others):
        pairs[t].wait()
        passing[t] += paired[t]
        copies.append(
            copy_to(2 * q + mine, passing.at[t], incoming.at[t], send_sems.at[t], recv_sems.at[t])
        )
    pairs[-1].wait()
    out[...] += paired[halves - 1]
    for t, copy in enumerate(copies):
        copy.wait()
        out[...] += incoming[t]


def local(n_space, n, multipole, inherited, send_rows, sources, operators):
    rows, width = multipole.shape
    count = operators.shape[0]
    slots, gh = send_rows.shape[1:]
    empty_row = rows + slots * gh
    held = -(-count // (2 * EACH)) * 2 * EACH
    safe = jnp.where(sources >= 0, 4 * sources, 4 * empty_row)
    safe = jnp.pad(safe, ((0, 0), (0, held - count)), constant_values=4 * empty_row)
    ids = safe.T.reshape(held // EACH, 1, EACH * rows)
    vmem = pl.BlockSpec(memory_space=pltpu.VMEM)
    smem = pl.BlockSpec(memory_space=pltpu.SMEM)
    chunk = rows // n
    dma = pltpu.SemaphoreType.DMA
    f32 = jnp.float32
    held_rows = -(-held // 8) * 8 * odd_stride(width)
    table, w_head, w_tail = pl.pallas_call(
        functools.partial(exchange, (n_space, slots // 2, gh)),
        in_specs=[smem, vmem, pl.BlockSpec(memory_space=pl.ANY)],
        out_specs=[vmem] * 3,
        out_shape=[
            jax.ShapeDtypeStruct((empty_row + 8, 4, LANES), f32),
            jax.ShapeDtypeStruct((held_rows, LANES), f32),
            jax.ShapeDtypeStruct((held_rows, LANES), f32),
        ],
        scratch_shapes=[
            pltpu.VMEM((rows, 2, LANES), f32),
            pltpu.VMEM((gh // 2, 2, LANES), f32),
            pltpu.VMEM((slots, gh // 2 + gh // 8, LANES), f32),
            pltpu.VMEM((slots, 2, gh // 2 + gh // 8, LANES), f32),
            pltpu.VMEM((width, width, count), f32),
            dma((PARTS,)),
            dma((slots,)),
            dma((slots,)),
            dma((slots,)),
            dma((slots,)),
        ],
        compiler_params=pltpu.CompilerParams(
            collective_id=0, has_side_effects=True, vmem_limit_bytes=28 * 1024 * 1024
        ),
        name="exchange",
    )(send_rows.reshape(-1), multipole.T, operators.transpose(1, 2, 0))
    total = pl.pallas_call(
        functools.partial(translate, width, count),
        in_specs=[vmem] * 4,
        out_specs=vmem,
        out_shape=jax.ShapeDtypeStruct((rows, 2 * LANES), f32),
        scratch_shapes=[
            pltpu.VMEM((4 * rows, LANES), f32),
            pltpu.VMEM((4 * rows, LANES), f32),
            pltpu.SMEM((EACH * rows,), jnp.int32),
            pltpu.SMEM((EACH * rows,), jnp.int32),
            dma((2,)),
        ],
        compiler_params=pltpu.CompilerParams(vmem_limit_bytes=16 * 1024 * 1024),
        name="translate",
    )(ids, table, w_head, w_tail)
    out = pl.pallas_call(
        functools.partial(reduce_scatter, n),
        in_specs=[vmem] * 2,
        out_specs=vmem,
        out_shape=jax.ShapeDtypeStruct((width, chunk), f32),
        scratch_shapes=[
            pltpu.VMEM((n // 2, width, chunk), f32),
            pltpu.VMEM((n // 2, width, chunk), f32),
            pltpu.VMEM((n // 2 - 1, width, chunk), f32),
            pltpu.VMEM((n // 2 - 1, width, chunk), f32),
            dma((n // 2,)),
            dma((n // 2,)),
            dma((n // 2 - 1,)),
            dma((n // 2 - 1,)),
        ],
        compiler_params=pltpu.CompilerParams(
            collective_id=1, has_side_effects=True, vmem_limit_bytes=8 * 1024 * 1024
        ),
        name="reduce_scatter",
    )(total, inherited.T)
    return out.T


def solution(mesh):
    return jax.shard_map(
        functools.partial(local, mesh.shape["space"], mesh.shape["sub"]),
        mesh=mesh,
        in_specs=(
            P("space", None),
            P(("space", "sub"), None),
            P("space", None, None),
            P("space", "sub"),
            P("sub", None, None),
        ),
        out_specs=P(("space", "sub"), None),
        check_vma=False,
    )
```
